128 devices in a mesh: dp: 16 (over y, z), sub: 8 (over x, core).
Axes of the slice: x: 4, y: 4, z: 4, core: 2. Of those that a mesh axis runs over, the one named last changes fastest.
Arguments:
- queries: bfloat16 [64, 64, 576], P('dp'), may hold values from -195 to 195
- own_cache: bfloat16 [64, 2048, 576], P('dp', 'sub'), may hold values from -8 to 8
- own_len: int32 [64, 8], P('dp', 'sub'), may hold values from 2 to 256
- host_cache: bfloat16 [16, 8, 16, 1024, 576], P('dp', 'sub'), may hold values from -8 to 8
- host_len: int32 [16, 8, 16], P('dp', 'sub'), may hold values from 2 to 1024
- page_plan: int32 [16, 8, 16], P('dp', 'sub'), may hold values from 0 to 3
- value_up: bfloat16 [64, 512, 128], P('sub'), may hold values from -0.25 to 0.25
Outputs:
- attended: bfloat16 [64, 64, 128], P('dp', 'sub')
The draws below stay inside these ranges and needn't reach their ends.
All inputs are finite; a program needn't handle non-finite values.
Results may differ from the reference program's by a relative error of at most 0.008.
Values may be sent and summed in bfloat16 or wider, within the bound.
A program may use at most 128 MiB of HBM per device.

```python
import jax
import jax.numpy as jnp
from jax import lax

H = 64
DL = 512
DR = 64
VD = 128
RG = 4
OWN_TOK = 256
HOST_TOK = 1024
B = 64
N_DP = 16
N_SUB = 8


def draw_page_plan(key, part):
    base = jax.random.fold_in(key, 11)
    earlier = jax.random.randint(jax.random.fold_in(base, 1), (N_DP, N_SUB, N_DP), 0, RG)
    later = jax.random.randint(jax.random.fold_in(base, 2), (N_DP, N_SUB, N_DP), 0, RG)
    ranked = jnp.minimum(earlier, later).astype(jnp.int32)
    ranks = jax.random.randint(jax.random.fold_in(base, 3), (N_DP, N_SUB, RG), 0, 1 << 20) * RG
    ranks = ranks + lax.broadcasted_iota(jnp.int32, (N_DP, N_SUB, RG), 2)
    ordering = jnp.argsort(ranks, axis=-1, stable=True).astype(jnp.int32)
    return jnp.take_along_axis(ordering, ranked, axis=-1).astype(jnp.int32)


def draw_queries(key, part):
    base = jax.random.fold_in(key, 31)
    values = jax.random.truncated_normal(jax.random.fold_in(base, 1), -4.0, 4.0, (N_DP * RG, H, DL + DR), jnp.float32)
    return values.astype(jnp.bfloat16)


def draw_own_cache(key, part):
    base = jax.random.fold_in(key, 21)
    noise = jax.random.truncated_normal(jax.random.fold_in(base, 1), -4.0, 4.0, (N_DP * RG, N_SUB, OWN_TOK, DL + DR), jnp.float32)
    centre = jax.random.truncated_normal(jax.random.fold_in(base, 2), -4.0, 4.0, (N_DP * RG, N_SUB, 1, DL), jnp.float32)
    latent = noise[..., :DL] + centre
    rotary = noise[..., DL:]
    whole = jnp.concatenate([latent, rotary], axis=-1)
    return whole.reshape(N_DP * RG, N_SUB * OWN_TOK, DL + DR).astype(jnp.bfloat16)


def draw_host_cache(key, part):
    base = jax.random.fold_in(key, 41)

    def one_helper(helper):
        inner = jax.random.fold_in(base, helper)
        noise = jax.random.truncated_normal(jax.random.fold_in(inner, 1), -4.0, 4.0, (N_SUB, N_DP, HOST_TOK, DL + DR), jnp.float32)
        centre = jax.random.truncated_normal(jax.random.fold_in(inner, 2), -4.0, 4.0, (N_SUB, N_DP, 1, DL), jnp.float32)
        latent = noise[..., :DL] + centre
        rotary = noise[..., DL:]
        return jnp.concatenate([latent, rotary], axis=-1).astype(jnp.bfloat16)
    return lax.map(one_helper, jnp.arange(N_DP, dtype=jnp.int32))


def place_ends(array, key, low, high):
    index_at = [jax.random.randint(jax.random.fold_in(key, axis), (), 0, length) for axis, length in enumerate(array.shape)]
    widest = array.shape.index(max(array.shape))
    neighbour = index_at[:widest] + [(index_at[widest] + 1) % array.shape[widest]] + index_at[widest + 1:]
    return array.at[tuple(index_at)].set(low).at[tuple(neighbour)].set(high)


def shard_levels(own_key, shape, shards, least, high):
    loudness = 1.0
    for dim, parts in shards:
        steps = jax.random.uniform(jax.random.fold_in(jax.random.fold_in(own_key, 6), dim), (parts,), jnp.float32, least / len(shards), high / len(shards))
        loudness = loudness * jnp.repeat(jnp.exp(steps), shape[dim] // parts).reshape((-1,) + (1,) * (len(shape) - 1 - dim))
    return loudness


def normal_values(key, extent, spread, most, pieces=(), kind=jnp.bfloat16):
    values = spread * jax.random.normal(key, extent, jnp.float32)
    if pieces:
        values = values * shard_levels(key, extent, pieces, -0.22, 0.18)
    return jnp.clip(values, -most, most).astype(kind)


def setup_inputs(seed: int = 0) -> dict:
    seeds = jax.random.split(jax.random.key(seed), 8)
    return {
        "queries": draw_queries(jax.random.fold_in(seeds[7], 71), 0),
        "own_cache": draw_own_cache(jax.random.fold_in(seeds[7], 71), 0),
        "own_len": place_ends(jax.random.randint(seeds[2], (B, N_SUB), 2, OWN_TOK + 1), jax.random.fold_in(seeds[2], 1), 2, OWN_TOK).astype(jnp.int32),
        "host_cache": draw_host_cache(jax.random.fold_in(seeds[7], 71), 0),
        "host_len": place_ends(jax.random.randint(seeds[4], (N_DP, N_SUB, N_DP), 2, HOST_TOK + 1), jax.random.fold_in(seeds[4], 1), 2, HOST_TOK).astype(jnp.int32),
        "page_plan": draw_page_plan(jax.random.fold_in(seeds[7], 71), 0),
        "value_up": normal_values(seeds[6], (H, DL, VD), DL ** -0.5, 0.25, ((0, 8),)),
    }


score_scale = 192 ** -0.5
masked_score = -1e30
highest = lax.Precision.HIGHEST


def attend(queries, slot_cache, lengths):
    query_wide = queries.astype(jnp.float32)
    cache_wide = slot_cache.astype(jnp.float32)
    scores = jnp.einsum("phd,ptd->pht", query_wide, cache_wide, precision=highest) * score_scale
    position = jnp.arange(slot_cache.shape[1], dtype=jnp.int32)
    scores = jnp.where(position[None, None, :] < lengths[:, None, None], scores, masked_score)
    largest = jnp.max(scores, axis=2, keepdims=True)
    exponent = jnp.exp(scores - largest)
    totals = jnp.sum(exponent, axis=2)
    weights = lax.optimization_barrier(exponent.astype(jnp.bfloat16)).astype(jnp.float32)
    weighted = jnp.einsum("pht,ptd->phd", weights, cache_wide[:, :, :DL], precision=highest)
    return weighted / totals[:, :, None], largest[:, :, 0] + jnp.log(totals)


def reference(queries, own_cache, own_len, host_cache, host_len, page_plan, value_up):
    width = DL + DR
    own_groups = own_cache.reshape(N_DP, RG * N_SUB, OWN_TOK, width)
    query_groups = queries.reshape(N_DP, RG, H, width)
    length_groups = own_len.reshape(N_DP, RG * N_SUB)

    def own_block(operands):
        group_queries, group_cache, group_lengths = operands
        return attend(jnp.repeat(group_queries, N_SUB, axis=0), group_cache, group_lengths)

    own_out, own_lse = lax.map(own_block, (query_groups, own_groups, length_groups))
    own_out = own_out.reshape(N_DP, RG, N_SUB, H, DL)
    own_lse = own_lse.reshape(N_DP, RG, N_SUB, H)
    owners = jnp.arange(N_DP, dtype=jnp.int32) * RG

    def host_block(operands):
        slot_cache, slot_lengths, slot_plan = operands
        index = (owners[None, :] + slot_plan).reshape(N_SUB * N_DP).astype(jnp.int32)
        return attend(queries[index], slot_cache.reshape(N_SUB * N_DP, HOST_TOK, width), slot_lengths.reshape(N_SUB * N_DP))

    plan_by_helper = jnp.transpose(page_plan, (2, 1, 0))
    host_out, host_lse = lax.map(host_block, (host_cache, host_len, plan_by_helper))
    host_out = jnp.transpose(host_out.reshape(N_DP, N_SUB, N_DP, H, DL), (2, 1, 0, 3, 4))
    host_lse = jnp.transpose(host_lse.reshape(N_DP, N_SUB, N_DP, H), (2, 1, 0, 3))
    matched = page_plan[..., None] == jnp.arange(RG, dtype=jnp.int32)
    masked = jnp.where(matched[..., None], host_lse[:, :, :, None, :], masked_score)
    largest = jnp.maximum(jnp.max(own_lse, axis=2), jnp.max(masked, axis=(1, 2)))
    own_weight = jnp.exp(own_lse - largest[:, :, None, :])
    help_weight = jnp.exp(masked - largest[:, None, None, :, :])
    summed = jnp.einsum("grsh,grshd->grhd", own_weight, own_out, precision=highest)
    summed = summed + jnp.einsum("gsprh,gsphd->grhd", help_weight, host_out, precision=highest)
    totals = jnp.sum(own_weight, axis=2) + jnp.sum(help_weight, axis=(1, 2))
    latent = (summed / totals[..., None]).astype(jnp.bfloat16).reshape(N_DP * RG, H, DL)
    result = jnp.einsum("bhd,hde->bhe", latent.astype(jnp.float32), value_up.astype(jnp.float32), precision=highest)
    return result.astype(jnp.bfloat16)
```

```python
import jax
import jax.numpy as jnp
from jax import lax
from jax.experimental import pallas as pl
from jax.experimental.pallas import tpu as pltpu
from jax.sharding import PartitionSpec as P

MESH = pl.DeviceIdType.MESH
DL = 512
scale2 = 192 ** (-0.5) * 1.4426950408889634
masked_score = -1e30


def offset(k):
    b, kk = k // 4, k % 4
    i = (kk + jnp.minimum(b, 1)) % 4
    return (2 * b) % 4 + b // 2, (2 * i) % 4 + i // 2


def attend(query, keys, length):
    scores = jnp.dot(query, keys, preferred_element_type=jnp.float32)
    position = lax.broadcasted_iota(jnp.int32, scores.shape, 1)
    scores = jnp.where(position < length, scores, masked_score)
    largest = jnp.max(scores, axis=1, keepdims=True)
    exponent = jnp.exp2((scores - largest) * scale2)
    total = jnp.sum(exponent, axis=1, keepdims=True)
    weighted = lax.dot_general(
        exponent.astype(jnp.bfloat16),
        keys[:DL],
        (((1,), (1,)), ((), ())),
        preferred_element_type=jnp.float32,
    )
    return weighted / total, largest * scale2 + jnp.log2(total)


def kernel(
    own_len,
    host_len,
    plan_s,
    plan_v,
    queries,
    own_hbm,
    host_hbm,
    value_up,
    out,
    own,
    cache,
    packed,
    q_out,
    q_in,
    plan_in,
    o_out,
    o_in,
    stat,
    s_out,
    s_in,
    latent,
    c_out,
    c_in,
    own_sem,
    cache_sem,
    qs_sem,
    qr_sem,
    ps_sem,
    pr_sem,
    os_sem,
    or_sem,
    ss_sem,
    sr_sem,
    cs_sem,
    cr_sem,
):
    dp, sub = lax.axis_index("dp"), lax.axis_index("sub")
    y, z = dp // 4, dp % 4

    def ahead(k):
        dy, dz = offset(k)
        return ((y + dy) % 4) * 4 + (z + dz) % 4

    def behind(k):
        dy, dz = offset(k)
        return ((y + 4 - dy) % 4) * 4 + (z + 4 - dz) % 4

    def cache_copy(k):
        return pltpu.make_async_copy(host_hbm.at[behind(k)], cache.at[k], cache_sem.at[k])

    def remote(source, target, send, receive, device):
        return pltpu.make_async_remote_copy(
            source, target, send, receive, device_id=device, device_id_type=MESH
        )

    own_copy = pltpu.make_async_copy(own_hbm, own, own_sem)
    own_copy.start()

    barrier = pltpu.get_barrier_semaphore()

    def greet_dp(k, carry):
        pl.semaphore_signal(barrier, inc=1, device_id=(ahead(k), sub), device_id_type=MESH)
        return carry

    def greet_sub(j, carry):
        pl.semaphore_signal(barrier, inc=1, device_id=(dp, (sub + j) % 8), device_id_type=MESH)
        return carry

    lax.fori_loop(1, 16, greet_dp, 0)
    lax.fori_loop(1, 8, greet_sub, 0)

    def fetch(k, carry):
        cache_copy(k).start()
        return carry

    lax.fori_loop(0, 16, fetch, 0)

    for r in range(4):
        for c in range(4):
            packed[r, 64 * c : 64 * c + 64, :] = queries[r, :, 128 * c : 128 * c + 128]
        packed[r, 256:288, :] = jnp.concatenate(
            [queries[r, :32, 512:576], queries[r, 32:, 512:576]], axis=1
        )

    q_in[0] = packed[plan_s[dp]]

    def select(k, carry):
        q_out[k] = packed[plan_s[ahead(k)]]
        return carry

    lax.fori_loop(1, 16, select, 0)

    lane = lax.broadcasted_iota(jnp.int32, (64, 128), 1)

    own_copy.wait()
    stat[...] = jnp.full((64, 128), masked_score, jnp.float32)

    def own_step(r, carry):
        weighted, lse = attend(queries[r], own[r], own_len[r])
        o_out[r] = weighted.astype(jnp.bfloat16).reshape(8, 8, DL)
        stat[...] = jnp.where(lane == 5 * r, lse, stat[...])
        return carry

    lax.fori_loop(0, 4, own_step, 0)

    pl.semaphore_wait(barrier, 22)

    def plan_copy(k):
        return remote(plan_v, plan_in.at[k], ps_sem.at[k], pr_sem.at[k], (ahead(k), sub))

    def query_copy(k):
        return remote(q_out.at[k], q_in.at[k], qs_sem.at[k], qr_sem.at[k], (ahead(k), sub))

    def send_query(k, carry):
        query_copy(k).start()
        plan_copy(k).start()
        return carry

    lax.fori_loop(1, 16, send_query, 0)
    plan_in[0] = plan_v[...]

    def send_unit(u):
        def one(j, carry):
            to = (sub + j) % 8
            remote(
                o_out.at[u, to], o_in.at[u, j - 1], os_sem.at[u], or_sem.at[u], (dp, to)
            ).start()
            return carry

        lax.fori_loop(1, 8, one, 0)

    def send_stat(b):
        s_out[b] = stat[...].reshape(8, 8, 128)

        def one(j, carry):
            to = (sub + j) % 8
            remote(
                s_out.at[b, to], s_in.at[b, j - 1], ss_sem.at[b], sr_sem.at[b], (dp, to)
            ).start()
            return carry

        lax.fori_loop(1, 8, one, 0)

    def send_own(u, carry):
        send_unit(u)
        return carry

    lax.fori_loop(0, 4, send_own, 0)
    send_stat(0)

    def step(k, kk):
        cache_copy(k).wait()

        @pl.when(k > 0)
        def _():
            query_copy(k).wait_recv()
            plan_copy(k).wait_recv()

        block = q_in[k]
        query = jnp.concatenate(
            [block[64 * c : 64 * c + 64] for c in range(4)]
            + [jnp.concatenate([block[256:288, :64], block[256:288, 64:]], axis=0)],
            axis=1,
        )
        weighted, lse = attend(query, cache[k], host_len[behind(k)])
        o_out[k + 4] = weighted.astype(jnp.bfloat16).reshape(8, 8, DL)
        lanes = lax.broadcasted_iota(jnp.int32, (1, 16), 1)
        request = jnp.sum(jnp.where(lanes == dp, plan_in[k], 0), axis=1, keepdims=True)
        stat[...] = jnp.where(lane == 4 * kk + request, lse, stat[...])
        send_unit(k + 4)

    def c_copy(k):
        return remote(c_out.at[k + 4], c_in.at[k], cs_sem.at[k], cr_sem.at[k], (behind(k), sub))

    def combine(b):
        def all_in(buffer, target, semaphore):
            return pltpu.make_async_copy(buffer.at[pl.ds(0, 7)], target, semaphore)

        all_in(s_out.at[b], s_in.at[b], sr_sem.at[b]).wait()
        for kk in range(4):
            u = 4 * b + kk
            all_in(o_out.at[u], o_in.at[u], or_sem.at[u]).wait()
        logs = [s_out[b, sub]] + [s_in[b, j] for j in range(7)]
        peak = logs[0]
        for value in logs[1:]:
            peak = jnp.maximum(peak, value)
        weights = [jnp.exp2(value - peak) for value in logs]
        total = weights[0]
        for value in weights[1:]:
            total = total + value
        lse = peak + jnp.log2(total)
        weights = [value / total for value in weights]
        for kk in range(4):
            u = 4 * b + kk
            sums = [jnp.zeros((8, DL), jnp.float32) for _ in range(4)]
            for j in range(8):
                piece = (o_out[u, sub] if j == 0 else o_in[u, j - 1]).astype(jnp.float32)
                for r in range(4):
                    at = 4 * kk + r
                    sums[r] = sums[r] + weights[j][:, at : at + 1] * piece
            for r in range(4):
                latent[4 * kk + r] = sums[r]
            c_out[u, 4] = lse if kk == 0 else pltpu.roll(lse, 128 - 4 * kk, 1)
        for h in range(8):
            rows = latent[:, h, :].astype(jnp.bfloat16)
            value = jnp.dot(rows, value_up[h], preferred_element_type=jnp.float32)
            for kk in range(4):
                c_out[4 * b + kk, 0:4, h, :] = value[4 * kk : 4 * kk + 4]

    def batch(b, carry):
        @pl.when(b < 4)
        def _():
            stat[...] = jnp.full((64, 128), masked_score, jnp.float32)

            def pair(i, carry):
                for t in range(2):
                    step(4 * b + 2 * i + t, 2 * i + t)
                return carry

            lax.fori_loop(0, 2, pair, 0)
            send_stat(b + 1)

        combine(b)

        @pl.when(b > 0)
        def _():
            def send(kk, carry):
                k = 4 * b - 4 + kk

                @pl.when(k > 0)
                def _():
                    c_copy(k).start()

                return carry

            lax.fori_loop(0, 4, send, 0)

        return carry

    lax.fori_loop(0, 5, batch, 0)

    def arrive(k, carry):
        c_copy(k).wait_recv()
        return carry

    lax.fori_loop(1, 16, arrive, 0)

    def contribution(u):
        return c_out.at[u] if u < 5 else c_in.at[u - 4]

    peak = contribution(0)[4]
    for u in range(1, 20):
        peak = jnp.maximum(peak, contribution(u)[4])
    total = jnp.zeros((8, 128), jnp.float32)
    sums = [jnp.zeros((8, 128), jnp.float32) for _ in range(4)]
    for u in range(20):
        weight = jnp.exp2(contribution(u)[4] - peak)
        total = total + weight
        for r in range(4):
            sums[r] = sums[r] + weight[:, r : r + 1] * contribution(u)[r]
    for r in range(4):
        out[r] = (sums[r] / total[:, r : r + 1]).astype(out.dtype)

    def finish(k, carry):
        query_copy(k).wait_send()
        plan_copy(k).wait_send()
        c_copy(k).wait_send()
        return carry

    lax.fori_loop(1, 16, finish, 0)

    def sent(u, carry):
        pltpu.make_async_copy(o_out.at[u, pl.ds(0, 7)], o_in.at[u], os_sem.at[u]).wait()
        return carry

    lax.fori_loop(0, 20, sent, 0)

    def sent_stat(b, carry):
        pltpu.make_async_copy(s_out.at[b, pl.ds(0, 7)], s_in.at[b], ss_sem.at[b]).wait()
        return carry

    lax.fori_loop(0, 5, sent_stat, 0)


def local(queries, own_cache, own_len, host_cache, host_len, page_plan, value_up):
    bf16, f32 = jnp.bfloat16, jnp.float32
    host = jnp.swapaxes(host_cache, 3, 4).reshape(16, 576, 1024)
    own = jnp.swapaxes(own_cache, 1, 2)
    vmem = pl.BlockSpec(memory_space=pltpu.VMEM)
    smem = pl.BlockSpec(memory_space=pltpu.SMEM)
    anywhere = pl.BlockSpec(memory_space=pl.ANY)
    dma = pltpu.SemaphoreType.DMA
    return pl.pallas_call(
        kernel,
        out_shape=jax.ShapeDtypeStruct((4, 8, 128), bf16),
        in_specs=[smem, smem, smem, vmem, vmem, anywhere, anywhere, vmem],
        out_specs=vmem,
        scratch_shapes=[
            pltpu.VMEM((4, 576, 256), bf16),
            pltpu.VMEM((16, 576, 1024), bf16),
            pltpu.VMEM((4, 288, 128), bf16),
            pltpu.VMEM((16, 288, 128), bf16),
            pltpu.VMEM((16, 288, 128), bf16),
            pltpu.VMEM((16, 1, 16), jnp.int32),
            pltpu.VMEM((20, 8, 8, DL), bf16),
            pltpu.VMEM((20, 7, 8, DL), bf16),
            pltpu.VMEM((64, 128), f32),
            pltpu.VMEM((5, 8, 8, 128), f32),
            pltpu.VMEM((5, 7, 8, 128), f32),
            pltpu.VMEM((16, 8, DL), f32),
            pltpu.VMEM((20, 5, 8, 128), f32),
            pltpu.VMEM((16, 5, 8, 128), f32),
            dma,
            dma((16,)),
            dma((16,)),
            dma((16,)),
            dma((16,)),
            dma((16,)),
            dma((20,)),
            dma((20,)),
            dma((5,)),
            dma((5,)),
            dma((16,)),
            dma((16,)),
        ],
        compiler_params=pltpu.CompilerParams(
            vmem_limit_bytes=60 * 2**20, collective_id=0, has_side_effects=True
        ),
    )(
        own_len.reshape(4),
        host_len.reshape(16),
        page_plan.reshape(16),
        page_plan.reshape(1, 16),
        queries,
        own,
        host,
        value_up,
    )


def solution(mesh):
    return jax.shard_map(
        local,
        mesh=mesh,
        in_specs=(
            P("dp", None, None),
            P("dp", "sub", None),
            P("dp", "sub"),
            P("dp", "sub", None, None, None),
            P("dp", "sub", None),
            P("dp", "sub", None),
            P("sub", None, None),
        ),
        out_specs=P("dp", "sub", None),
        check_vma=False,
    )
```

```python
import jax
import jax.numpy as jnp
from jax import lax
from jax.experimental import pallas as pl
from jax.experimental.pallas import tpu as pltpu
from jax.sharding import PartitionSpec as P

MESH = pl.DeviceIdType.MESH
DL = 512
scale2 = 192 ** (-0.5) * 1.4426950408889634
masked_score = -1e30


STEPS = [(0, 0), (2, 2), (2, 3), (3, 2), (2, 1), (1, 2), (2, 0), (0, 2)]
STEPS += [(3, 1), (1, 3), (3, 3), (1, 1), (3, 0), (0, 3), (1, 0), (0, 1)]


def offset(k):
    if isinstance(k, int):
        return STEPS[k]
    words = [sum(step[i] << (2 * n) for n, step in enumerate(STEPS)) for i in range(2)]
    words = [jnp.int32(word - (1 << 32) if word >= 1 << 31 else word) for word in words]
    return tuple(lax.shift_right_logical(word, 2 * k) & 3 for word in words)


def score(query, keys):
    return jnp.dot(query, keys, preferred_element_type=jnp.float32)


def attend(scores, keys, length):
    position = lax.broadcasted_iota(jnp.int32, scores.shape, 1)
    scores = jnp.where(position < length, scores, masked_score)
    largest = jnp.max(scores, axis=1, keepdims=True)
    exponent = jnp.exp2((scores - largest) * scale2)
    total = jnp.sum(exponent, axis=1, keepdims=True)
    weighted = lax.dot_general(
        exponent.astype(jnp.bfloat16),
        keys[:DL],
        (((1,), (1,)), ((), ())),
        preferred_element_type=jnp.float32,
    )
    return weighted / total, largest * scale2 + jnp.log2(total)


def kernel(
    own_len,
    host_len,
    plan_s,
    plan_v,
    queries_hbm,
    own_hbm,
    host_hbm,
    value_hbm,
    out,
    queries,
    value_up,
    own,
    cache,
    packed,
    q_out,
    q_in,
    plan_in,
    o_out,
    o_in,
    stat,
    s_out,
    s_in,
    score_buffer,
    latent,
    c_out,
    c_in,
    query_sem,
    value_sem,
    own_sem,
    cache_sem,
    qs_sem,
    qr_sem,
    ps_sem,
    pr_sem,
    os_sem,
    or_sem,
    ss_sem,
    sr_sem,
    cs_sem,
    cr_sem,
):
    dp, sub = lax.axis_index("dp"), lax.axis_index("sub")
    y, z = dp // 4, dp % 4

    def ahead(k):
        dy, dz = offset(k)
        return ((y + dy) & 3) * 4 + ((z + dz) & 3)

    def behind(k):
        dy, dz = offset(k)
        return ((y + 4 - dy) & 3) * 4 + ((z + 4 - dz) & 3)

    def peer(j):
        return (sub + j) & 7

    def cache_copy(k):
        return pltpu.make_async_copy(host_hbm.at[behind(k)], cache.at[k], cache_sem.at[k])

    def remote(source, target, send, receive, device):
        return pltpu.make_async_remote_copy(
            source, target, send, receive, device_id=device, device_id_type=MESH
        )

    query_fetch = pltpu.make_async_copy(queries_hbm, queries, query_sem)
    query_fetch.start()
    own_copy = pltpu.make_async_copy(own_hbm, own, own_sem)
    own_copy.start()
    barrier = pltpu.get_barrier_semaphore()
    for k in range(1, 16):
        pl.semaphore_signal(barrier, inc=1, device_id=(ahead(k), sub), device_id_type=MESH)
    for j in range(1, 8):
        pl.semaphore_signal(barrier, inc=1, device_id=(dp, peer(j)), device_id_type=MESH)

    def fetch(k, carry):
        cache_copy(k).start()
        return carry

    lax.fori_loop(0, 16, fetch, 0)
    value_copy = pltpu.make_async_copy(value_hbm, value_up, value_sem)
    value_copy.start()

    query_fetch.wait()
    for r in range(4):
        for c in range(4):
            packed[r, 64 * c : 64 * c + 64, :] = queries[r, :, 128 * c : 128 * c + 128]
        packed[r, 256:288, :] = jnp.concatenate(
            [queries[r, :32, 512:576], queries[r, 32:, 512:576]], axis=1
        )

    def select(k, carry):
        q_out[k] = packed[plan_s[ahead(k)]]
        return carry

    lax.fori_loop(1, 16, select, 0)

    def plan_copy(k):
        return remote(plan_v, plan_in.at[k], ps_sem.at[k], pr_sem.at[k], (ahead(k), sub))

    def query_copy(k):
        return remote(q_out.at[k], q_in.at[k], qs_sem.at[k], qr_sem.at[k], (ahead(k), sub))

    pl.semaphore_wait(barrier, 22)

    def send_query(k, carry):
        query_copy(k).start()
        return carry

    def send_plan(k, carry):
        plan_copy(k).start()
        return carry

    lax.fori_loop(1, 16, send_plan, 0)
    lax.fori_loop(1, 16, send_query, 0)

    q_in[0] = packed[plan_s[dp]]
    plan_in[0] = plan_v[...]

    def send_unit(u):
        for j in range(1, 8):
            to = peer(j)
            remote(
                o_out.at[u, to], o_in.at[u, j - 1], os_sem.at[u], or_sem.at[u], (dp, to)
            ).start()

    def send_stat(b):
        s_out[b] = stat[...].reshape(8, 8, 128)
        for j in range(1, 8):
            to = peer(j)
            remote(
                s_out.at[b, to], s_in.at[b, j - 1], ss_sem.at[b], sr_sem.at[b], (dp, to)
            ).start()
        stat[...] = jnp.full((64, 128), masked_score, jnp.float32)

    lane = lax.broadcasted_iota(jnp.int32, (64, 128), 1)

    own_copy.wait()
    stat[...] = jnp.full((64, 128), masked_score, jnp.float32)

    def own_step(r, carry):
        weighted, lse = attend(score(queries[r], own[r]), own[r], own_len[r])
        o_out[r] = weighted.astype(jnp.bfloat16).reshape(8, 8, DL)
        stat[...] = jnp.where(lane == 5 * r, lse, stat[...])
        send_unit(r)
        return carry

    lax.fori_loop(0, 4, own_step, 0)
    send_stat(0)

    def prepare(k):
        cache_copy(k).wait()

        @pl.when(k > 0)
        def _():
            query_copy(k).wait_recv()
            plan_copy(k).wait_recv()

    def score_step(k):
        block = q_in[k]
        query = jnp.concatenate(
            [block[64 * c : 64 * c + 64] for c in range(4)]
            + [jnp.concatenate([block[256:288, :64], block[256:288, 64:]], axis=0)],
            axis=1,
        )
        return score(query, cache[k])

    def step(k, t, last):
        if not last:
            prepare(k + 1)
            scores = score_buffer[t]
            score_buffer[1 - t] = score_step(k + 1)
        else:
            scores = score_buffer[t]
        weighted, lse = attend(scores, cache[k], host_len[behind(k)])
        o_out[k + 4] = weighted.astype(jnp.bfloat16).reshape(8, 8, DL)
        lanes = lax.broadcasted_iota(jnp.int32, (1, 16), 1)
        request = jnp.sum(jnp.where(lanes == dp, plan_in[k], 0), axis=1, keepdims=True)
        stat[...] = jnp.where(lane == 4 * (k % 4) + request, lse, stat[...])
        send_unit(k + 4)

    def c_copy(k):
        return remote(c_out.at[k + 4], c_in.at[k], cs_sem.at[k], cr_sem.at[k], (behind(k), sub))

    def combine(b):
        def all_in(buffer, target, semaphore):
            return pltpu.make_async_copy(buffer.at[pl.ds(0, 7)], target, semaphore)

        all_in(s_out.at[b], s_in.at[b], sr_sem.at[b]).wait()
        for kk in range(4):
            u = 4 * b + kk
            all_in(o_out.at[u], o_in.at[u], or_sem.at[u]).wait()
        logs = [s_out[b, sub]] + [s_in[b, j] for j in range(7)]
        peak = logs[0]
        for value in logs[1:]:
            peak = jnp.maximum(peak, value)
        weights = [jnp.exp2(value - peak) for value in logs]
        total = weights[0]
        for value in weights[1:]:
            total = total + value
        lse = peak + jnp.log2(total)
        weights = [value / total for value in weights]
        for kk in range(4):
            u = 4 * b + kk
            sums = [jnp.zeros((8, DL), jnp.float32) for _ in range(4)]
            for j in range(8):
                piece = (o_out[u, sub] if j == 0 else o_in[u, j - 1]).astype(jnp.float32)
                for r in range(4):
                    at = 4 * kk + r
                    sums[r] = sums[r] + weights[j][:, at : at + 1] * piece
            for r in range(4):
                latent[4 * kk + r] = sums[r]
            c_out[u, 4] = lse if kk == 0 else pltpu.roll(lse, 128 - 4 * kk, 1)
        for h in range(8):
            rows = latent[:, h, :].astype(jnp.bfloat16)
            value = jnp.dot(rows, value_up[h], preferred_element_type=jnp.float32)
            for kk in range(4):
                c_out[4 * b + kk, 0:4, h, :] = value[4 * kk : 4 * kk + 4]

    def send_back(b):
        for kk in range(4):
            k = 4 * b - 4 + kk

            @pl.when(k > 0)
            def _():
                c_copy(k).start()

    prepare(0)
    score_buffer[0] = score_step(0)
    value_copy.wait()

    def pair(i, carry):
        for t in range(2):
            step(2 * i + t, t, False)

        @pl.when(i % 2 == 1)
        def _():
            send_stat(i // 2 + 1)

        @pl.when((i % 2 == 0) & (i > 0))
        def _():
            combine(i // 2 - 1)
            send_back(i // 2 - 1)

        return carry

    lax.fori_loop(0, 7, pair, 0)
    step(14, 0, False)
    step(15, 1, True)
    send_stat(4)
    combine(3)
    send_back(3)
    combine(4)
    send_back(4)

    def arrive(k, carry):
        c_copy(k).wait_recv()
        return carry

    lax.fori_loop(1, 16, arrive, 0)

    def contribution(u):
        return c_out.at[u] if u < 5 else c_in.at[u - 4]

    peak = contribution(0)[4]
    for u in range(1, 20):
        peak = jnp.maximum(peak, contribution(u)[4])
    total = jnp.zeros((8, 128), jnp.float32)
    sums = [jnp.zeros((8, 128), jnp.float32) for _ in range(4)]
    for u in range(20):
        weight = jnp.exp2(contribution(u)[4] - peak)
        total = total + weight
        for r in range(4):
            sums[r] = sums[r] + weight[:, r : r + 1] * contribution(u)[r]
    for r in range(4):
        out[r] = (sums[r] / total[:, r : r + 1]).astype(out.dtype)

    def finish(k, carry):
        query_copy(k).wait_send()
        plan_copy(k).wait_send()
        c_copy(k).wait_send()
        return carry

    lax.fori_loop(1, 16, finish, 0)

    def sent(u, carry):
        pltpu.make_async_copy(o_out.at[u, pl.ds(0, 7)], o_in.at[u], os_sem.at[u]).wait()
        return carry

    lax.fori_loop(0, 20, sent, 0)

    def sent_stat(b, carry):
        pltpu.make_async_copy(s_out.at[b, pl.ds(0, 7)], s_in.at[b], ss_sem.at[b]).wait()
        return carry

    lax.fori_loop(0, 5, sent_stat, 0)


def local(queries, own_cache, own_len, host_cache, host_len, page_plan, value_up):
    bf16, f32 = jnp.bfloat16, jnp.float32
    host = jnp.swapaxes(host_cache, 3, 4).reshape(16, 576, 1024)
    own = jnp.swapaxes(own_cache, 1, 2)
    vmem = pl.BlockSpec(memory_space=pltpu.VMEM)
    smem = pl.BlockSpec(memory_space=pltpu.SMEM)
    anywhere = pl.BlockSpec(memory_space=pl.ANY)
    dma = pltpu.SemaphoreType.DMA
    return pl.pallas_call(
        kernel,
        out_shape=jax.ShapeDtypeStruct((4, 8, 128), bf16),
        in_specs=[smem, smem, smem, vmem, anywhere, anywhere, anywhere, anywhere],
        out_specs=vmem,
        scratch_shapes=[
            pltpu.VMEM((4, 64, 576), bf16),
            pltpu.VMEM((8, DL, 128), bf16),
            pltpu.VMEM((4, 576, 256), bf16),
            pltpu.VMEM((16, 576, 1024), bf16),
            pltpu.VMEM((4, 288, 128), bf16),
            pltpu.VMEM((16, 288, 128), bf16),
            pltpu.VMEM((16, 288, 128), bf16),
            pltpu.VMEM((16, 1, 16), jnp.int32),
            pltpu.VMEM((20, 8, 8, DL), bf16),
            pltpu.VMEM((20, 7, 8, DL), bf16),
            pltpu.VMEM((64, 128), f32),
            pltpu.VMEM((5, 8, 8, 128), f32),
            pltpu.VMEM((5, 7, 8, 128), f32),
            pltpu.VMEM((2, 64, 1024), f32),
            pltpu.VMEM((16, 8, DL), f32),
            pltpu.VMEM((20, 5, 8, 128), f32),
            pltpu.VMEM((16, 5, 8, 128), f32),
            dma,
            dma,
            dma,
            dma((16,)),
            dma((16,)),
            dma((16,)),
            dma((16,)),
            dma((16,)),
            dma((20,)),
            dma((20,)),
            dma((5,)),
            dma((5,)),
            dma((16,)),
            dma((16,)),
        ],
        compiler_params=pltpu.CompilerParams(
            vmem_limit_bytes=60 * 2**20, collective_id=0, has_side_effects=True
        ),
    )(
        own_len.reshape(4),
        host_len.reshape(16),
        page_plan.reshape(16),
        page_plan.reshape(1, 16),
        queries,
        own,
        host,
        value_up,
    )


def solution(mesh):
    return jax.shard_map(
        local,
        mesh=mesh,
        in_specs=(
            P("dp", None, None),
            P("dp", "sub", None),
            P("dp", "sub"),
            P("dp", "sub", None, None, None),
            P("dp", "sub", None),
            P("dp", "sub", None),
            P("sub", None, None),
        ),
        out_specs=P("dp", "sub", None),
        check_vma=False,
    )
```

```python
import jax
import jax.numpy as jnp
from jax import lax
from jax.experimental import pallas as pl
from jax.experimental.pallas import tpu as pltpu
from jax.sharding import PartitionSpec as P

MESH = pl.DeviceIdType.MESH
DL = 512
scale2 = 192 ** (-0.5) * 1.4426950408889634
masked_score = -1e30


STEPS = [(0, 0), (2, 2), (2, 3), (3, 2), (2, 1), (1, 2), (2, 0), (0, 2)]
STEPS += [(3, 1), (1, 3), (3, 3), (1, 1), (3, 0), (0, 3), (1, 0), (0, 1)]


def offset(k):
    if isinstance(k, int):
        return STEPS[k]
    words = [sum(step[i] << (2 * n) for n, step in enumerate(STEPS)) for i in range(2)]
    words = [jnp.int32(word - (1 << 32) if word >= 1 << 31 else word) for word in words]
    return tuple(lax.shift_right_logical(word, 2 * k) & 3 for word in words)


def score(query, keys):
    return jnp.dot(query, keys, preferred_element_type=jnp.float32)


def attend(scores, keys, length):
    position = lax.broadcasted_iota(jnp.int32, scores.shape, 1)
    scores = jnp.where(position < length, scores, masked_score)
    largest = jnp.max(scores, axis=1, keepdims=True)
    exponent = jnp.exp2((scores - largest) * scale2)
    total = jnp.sum(exponent, axis=1, keepdims=True)
    weighted = lax.dot_general(
        exponent.astype(jnp.bfloat16),
        keys[:DL],
        (((1,), (1,)), ((), ())),
        preferred_element_type=jnp.float32,
    )
    return weighted / total, largest * scale2 + jnp.log2(total)


def kernel(
    own_len,
    host_len,
    plan_s,
    plan_v,
    queries_hbm,
    own_hbm,
    host_hbm,
    value_hbm,
    out,
    queries,
    value_up,
    own,
    cache,
    packed,
    q_out,
    q_in,
    plan_in,
    o_out,
    o_in,
    stat,
    s_out,
    s_in,
    score_buffer,
    latent,
    c_out,
    c_in,
    query_sem,
    value_sem,
    own_sem,
    cache_sem,
    qs_sem,
    qr_sem,
    ps_sem,
    pr_sem,
    os_sem,
    or_sem,
    ss_sem,
    sr_sem,
    cs_sem,
    cr_sem,
):
    dp, sub = lax.axis_index("dp"), lax.axis_index("sub")
    y, z = dp // 4, dp % 4

    def ahead(k):
        dy, dz = offset(k)
        return ((y + dy) & 3) * 4 + ((z + dz) & 3)

    def behind(k):
        dy, dz = offset(k)
        return ((y + 4 - dy) & 3) * 4 + ((z + 4 - dz) & 3)

    def peer(j):
        return (sub + j) & 7

    def cache_copy(k):
        return pltpu.make_async_copy(host_hbm.at[behind(k)], cache.at[k], cache_sem.at[k])

    def remote(source, target, send, receive, device):
        return pltpu.make_async_remote_copy(
            source, target, send, receive, device_id=device, device_id_type=MESH
        )

    query_fetch = pltpu.make_async_copy(queries_hbm, queries, query_sem)
    query_fetch.start()
    own_copy = pltpu.make_async_copy(own_hbm, own, own_sem)
    own_copy.start()
    barrier = pltpu.get_barrier_semaphore()
    for k in range(1, 16):
        pl.semaphore_signal(barrier, inc=1, device_id=(ahead(k), sub), device_id_type=MESH)
    for j in range(1, 8):
        pl.semaphore_signal(barrier, inc=1, device_id=(dp, peer(j)), device_id_type=MESH)

    def fetch(k, carry):
        cache_copy(k).start()
        return carry

    lax.fori_loop(0, 16, fetch, 0)

    def value_copy(h):
        half = value_up.at[h // 2, :, 128 * (h % 2) : 128 * (h % 2) + 128]
        return pltpu.make_async_copy(value_hbm.at[h], half, value_sem.at[h])

    for h in range(8):
        value_copy(h).start()

    def value_wait():
        for h in range(8):
            value_copy(h).wait()

    o_out[4] = jnp.zeros((8, 8, DL), jnp.bfloat16)
    o_in[4] = jnp.zeros((7, 8, DL), jnp.bfloat16)

    query_fetch.wait()
    for r in range(4):
        for c in range(4):
            packed[r, 64 * c : 64 * c + 64, :] = queries[r, :, 128 * c : 128 * c + 128]
        packed[r, 256:288, :] = jnp.concatenate(
            [queries[r, :32, 512:576], queries[r, 32:, 512:576]], axis=1
        )

    def select(k, carry):
        q_out[k] = packed[plan_s[ahead(k)]]
        return carry

    lax.fori_loop(1, 16, select, 0)

    def plan_copy(k):
        return remote(plan_v, plan_in.at[k], ps_sem.at[k], pr_sem.at[k], (ahead(k), sub))

    def query_copy(k):
        return remote(q_out.at[k], q_in.at[k], qs_sem.at[k], qr_sem.at[k], (ahead(k), sub))

    pl.semaphore_wait(barrier, 22)

    def send_query(k, carry):
        query_copy(k).start()
        return carry

    def send_plan(k, carry):
        plan_copy(k).start()
        return carry

    lax.fori_loop(1, 16, send_plan, 0)
    lax.fori_loop(1, 16, send_query, 0)

    q_in[0] = packed[plan_s[dp]]
    plan_in[0] = plan_v[...]

    def send_unit(u):
        for j in range(1, 8):
            to = peer(j)
            remote(
                o_out.at[u, to], o_in.at[u, j - 1], os_sem.at[u], or_sem.at[u], (dp, to)
            ).start()

    def send_stat(b):
        s_out[b] = stat[...].reshape(8, 8, 128)
        for j in range(1, 8):
            to = peer(j)
            remote(
                s_out.at[b, to], s_in.at[b, j - 1], ss_sem.at[b], sr_sem.at[b], (dp, to)
            ).start()
        stat[...] = jnp.full((64, 128), masked_score, jnp.float32)

    lane = lax.broadcasted_iota(jnp.int32, (64, 128), 1)

    own_copy.wait()
    stat[...] = jnp.full((64, 128), masked_score, jnp.float32)

    def own_step(r, carry):
        weighted, lse = attend(score(queries[r], own[r]), own[r], own_len[r])
        o_out[r] = weighted.astype(jnp.bfloat16).reshape(8, 8, DL)
        stat[...] = jnp.where(lane == 5 * r, lse, stat[...])
        send_unit(r)
        return carry

    lax.fori_loop(0, 4, own_step, 0)
    send_stat(0)

    def prepare(k):
        cache_copy(k).wait()

        @pl.when(k > 0)
        def _():
            query_copy(k).wait_recv()
            plan_copy(k).wait_recv()

    def score_step(k):
        block = q_in[k]
        query = jnp.concatenate(
            [block[64 * c : 64 * c + 64] for c in range(4)]
            + [jnp.concatenate([block[256:288, :64], block[256:288, 64:]], axis=0)],
            axis=1,
        )
        return score(query, cache[k])

    def step(k, t, last):
        if not last:
            prepare(k + 1)
            scores = score_buffer[t]
            score_buffer[1 - t] = score_step(k + 1)
        else:
            scores = score_buffer[t]
        weighted, lse = attend(scores, cache[k], host_len[behind(k)])
        o_out[k + 5] = weighted.astype(jnp.bfloat16).reshape(8, 8, DL)
        lanes = lax.broadcasted_iota(jnp.int32, (1, 16), 1)
        request = jnp.sum(jnp.where(lanes == dp, plan_in[k], 0), axis=1, keepdims=True)
        stat[...] = jnp.where(lane == 4 * ((k + 1) % 4) + request, lse, stat[...])
        send_unit(k + 5)

    def c_copy(k):
        return remote(c_out.at[k + 5], c_in.at[k], cs_sem.at[k], cr_sem.at[k], (behind(k), sub))

    def combine(b, count=4):
        def all_in(buffer, target, semaphore):
            return pltpu.make_async_copy(buffer.at[pl.ds(0, 7)], target, semaphore)

        all_in(s_out.at[b], s_in.at[b], sr_sem.at[b]).wait()
        for kk in range(count):
            u = 4 * b + kk

            @pl.when(u != 4)
            def _():
                all_in(o_out.at[u], o_in.at[u], or_sem.at[u]).wait()

        logs = [s_out[b, sub]] + [s_in[b, j] for j in range(7)]
        peak = logs[0]
        for value in logs[1:]:
            peak = jnp.maximum(peak, value)
        weights = [jnp.exp2(value - peak) for value in logs]
        total = weights[0]
        for value in weights[1:]:
            total = total + value
        lse = peak + jnp.log2(total)
        weights = [value / total for value in weights]
        for kk in range(count):
            u = 4 * b + kk
            sums = [jnp.zeros((8, DL), jnp.float32) for _ in range(4)]
            for j in range(8):
                piece = (o_out[u, sub] if j == 0 else o_in[u, j - 1]).astype(jnp.float32)
                for r in range(4):
                    at = 4 * kk + r
                    sums[r] = sums[r] + weights[j][:, at : at + 1] * piece
            for r in range(4):
                latent[4 * kk + r] = sums[r]
            c_out[u, 4] = lse if kk == 0 else pltpu.roll(lse, 128 - 4 * kk, 1)
        rows = 4 * count
        for h in range(0, 8, 2):
            both = jnp.concatenate([latent[:rows, h, :], latent[:rows, h + 1, :]], axis=0)
            value = jnp.dot(
                both.astype(jnp.bfloat16), value_up[h // 2], preferred_element_type=jnp.float32
            )
            for kk in range(count):
                at = 4 * kk
                c_out[4 * b + kk, 0:4, h, :] = value[at : at + 4, :128]
                c_out[4 * b + kk, 0:4, h + 1, :] = value[rows + at : rows + at + 4, 128:]

    def send_back(b, count=4):
        for kk in range(count):
            k = 4 * b + kk - 5

            @pl.when(k > 0)
            def _():
                c_copy(k).start()

    cache_copy(0).wait()
    score_buffer[0] = score_step(0)
    step(0, 0, True)
    for k in (1, 2):
        prepare(k)
        score_buffer[0] = score_step(k)
        step(k, 0, True)
    send_stat(1)
    value_wait()
    combine(0)
    prepare(3)
    score_buffer[1] = score_step(3)

    def pair(i, carry):
        step(2 * i + 1, 1, False)
        step(2 * i + 2, 0, False)

        @pl.when(i % 2 == 0)
        def _():
            send_stat(i // 2 + 1)

        return carry

    lax.fori_loop(1, 7, pair, 0)
    step(15, 1, True)
    send_stat(5)

    def late(b, carry):
        combine(b)
        send_back(b)
        return carry

    lax.fori_loop(1, 5, late, 0)
    combine(5, 1)
    send_back(5, 1)

    def finish(k, carry):
        query_copy(k).wait_send()
        plan_copy(k).wait_send()
        return carry

    lax.fori_loop(1, 16, finish, 0)

    def sent(u, carry):
        @pl.when(u != 4)
        def _():
            pltpu.make_async_copy(o_out.at[u, pl.ds(0, 7)], o_in.at[u], os_sem.at[u]).wait()

        return carry

    lax.fori_loop(0, 21, sent, 0)

    def sent_stat(b, carry):
        pltpu.make_async_copy(s_out.at[b, pl.ds(0, 7)], s_in.at[b], ss_sem.at[b]).wait()
        return carry

    lax.fori_loop(0, 6, sent_stat, 0)

    def arrive(k, carry):
        c_copy(k).wait()
        return carry

    lax.fori_loop(1, 16, arrive, 0)

    parts = [c_out.at[u] for u in (0, 1, 2, 3, 5)] + [c_in.at[k] for k in range(1, 16)]
    peak = parts[0][4]
    for part in parts[1:]:
        peak = jnp.maximum(peak, part[4])
    total = jnp.zeros((8, 128), jnp.float32)
    sums = [jnp.zeros((8, 128), jnp.float32) for _ in range(4)]
    for part in parts:
        weight = jnp.exp2(part[4] - peak)
        total = total + weight
        for r in range(4):
            sums[r] = sums[r] + weight[:, r : r + 1] * part[r]
    for r in range(4):
        out[r] = (sums[r] / total[:, r : r + 1]).astype(out.dtype)


def local(queries, own_cache, own_len, host_cache, host_len, page_plan, value_up):
    bf16, f32 = jnp.bfloat16, jnp.float32
    host = jnp.swapaxes(host_cache, 3, 4).reshape(16, 576, 1024)
    own = jnp.swapaxes(own_cache, 1, 2)
    vmem = pl.BlockSpec(memory_space=pltpu.VMEM)
    smem = pl.BlockSpec(memory_space=pltpu.SMEM)
    anywhere = pl.BlockSpec(memory_space=pl.ANY)
    dma = pltpu.SemaphoreType.DMA
    return pl.pallas_call(
        kernel,
        out_shape=jax.ShapeDtypeStruct((4, 8, 128), bf16),
        in_specs=[smem, smem, smem, vmem, anywhere, anywhere, anywhere, anywhere],
        out_specs=vmem,
        scratch_shapes=[
            pltpu.VMEM((4, 64, 576), bf16),
            pltpu.VMEM((4, DL, 256), bf16),
            pltpu.VMEM((4, 576, 256), bf16),
            pltpu.VMEM((16, 576, 1024), bf16),
            pltpu.VMEM((4, 288, 128), bf16),
            pltpu.VMEM((16, 288, 128), bf16),
            pltpu.VMEM((16, 288, 128), bf16),
            pltpu.VMEM((16, 1, 16), jnp.int32),
            pltpu.VMEM((21, 8, 8, DL), bf16),
            pltpu.VMEM((21, 7, 8, DL), bf16),
            pltpu.VMEM((64, 128), f32),
            pltpu.VMEM((6, 8, 8, 128), f32),
            pltpu.VMEM((6, 7, 8, 128), f32),
            pltpu.VMEM((2, 64, 1024), f32),
            pltpu.VMEM((16, 8, DL), f32),
            pltpu.VMEM((24, 5, 8, 128), f32),
            pltpu.VMEM((16, 5, 8, 128), f32),
            dma,
            dma((8,)),
            dma,
            dma((16,)),
            dma((16,)),
            dma((16,)),
            dma((16,)),
            dma((16,)),
            dma((21,)),
            dma((21,)),
            dma((6,)),
            dma((6,)),
            dma((16,)),
            dma((16,)),
        ],
        compiler_params=pltpu.CompilerParams(
            vmem_limit_bytes=60 * 2**20, collective_id=0, has_side_effects=True
        ),
    )(
        own_len.reshape(4),
        host_len.reshape(16),
        page_plan.reshape(16),
        page_plan.reshape(1, 16),
        queries,
        own,
        host,
        value_up,
    )


def solution(mesh):
    return jax.shard_map(
        local,
        mesh=mesh,
        in_specs=(
            P("dp", None, None),
            P("dp", "sub", None),
            P("dp", "sub"),
            P("dp", "sub", None, None, None),
            P("dp", "sub", None),
            P("dp", "sub", None),
            P("sub", None, None),
        ),
        out_specs=P("dp", "sub", None),
        check_vma=False,
    )
```

```python
import jax
import jax.numpy as jnp
from jax import lax
from jax.experimental import pallas as pl
from jax.experimental.pallas import tpu as pltpu
from jax.sharding import PartitionSpec as P

MESH = pl.DeviceIdType.MESH
DL = 512
scale2 = 192 ** (-0.5) * 1.4426950408889634
masked_score = -1e30


STEPS = [(0, 0), (2, 2), (2, 3), (3, 2), (2, 1), (1, 2), (2, 0), (0, 2)]
STEPS += [(3, 1), (1, 3), (3, 3), (1, 1), (3, 0), (0, 3), (1, 0), (0, 1)]


def offset(k):
    if isinstance(k, int):
        return STEPS[k]
    words = [sum(step[i] << (2 * n) for n, step in enumerate(STEPS)) for i in range(2)]
    words = [jnp.int32(word - (1 << 32) if word >= 1 << 31 else word) for word in words]
    return tuple(lax.shift_right_logical(word, 2 * k) & 3 for word in words)


def score(query, keys):
    return jnp.dot(query, keys, preferred_element_type=jnp.float32)


def attend(scores, keys, length):
    position = lax.broadcasted_iota(jnp.int32, scores.shape, 1)
    scores = jnp.where(position < length, scores, masked_score)
    largest = jnp.max(scores, axis=1, keepdims=True)
    exponent = jnp.exp2((scores - largest) * scale2)
    total = jnp.sum(exponent, axis=1, keepdims=True)
    weighted = lax.dot_general(
        exponent.astype(jnp.bfloat16),
        keys[:DL],
        (((1,), (1,)), ((), ())),
        preferred_element_type=jnp.float32,
    )
    return weighted / total, largest * scale2 + jnp.log2(total)


def kernel(
    own_len,
    host_len,
    plan_s,
    plan_v,
    queries_hbm,
    own_hbm,
    host_hbm,
    value_hbm,
    out,
    queries,
    value_up,
    own,
    cache,
    packed,
    q_out,
    q_in,
    plan_in,
    o_out,
    o_in,
    stat,
    s_out,
    s_in,
    score_buffer,
    latent,
    result,
    c_out,
    c_in,
    query_sem,
    value_sem,
    own_sem,
    cache_sem,
    qs_sem,
    qr_sem,
    ps_sem,
    pr_sem,
    os_sem,
    or_sem,
    ss_sem,
    sr_sem,
    cs_sem,
    cr_sem,
):
    dp, sub = lax.axis_index("dp"), lax.axis_index("sub")
    y, z = dp // 4, dp % 4

    def ahead(k):
        dy, dz = offset(k)
        return ((y + dy) & 3) * 4 + ((z + dz) & 3)

    def behind(k):
        dy, dz = offset(k)
        return ((y + 4 - dy) & 3) * 4 + ((z + 4 - dz) & 3)

    def peer(j):
        return (sub + j) & 7

    def cache_copy(k):
        return pltpu.make_async_copy(host_hbm.at[behind(k)], cache.at[k], cache_sem.at[k])

    def remote(source, target, send, receive, device):
        return pltpu.make_async_remote_copy(
            source, target, send, receive, device_id=device, device_id_type=MESH
        )

    query_fetch = pltpu.make_async_copy(queries_hbm, queries, query_sem)
    query_fetch.start()
    own_copy = pltpu.make_async_copy(own_hbm, own, own_sem)
    own_copy.start()
    barrier = pltpu.get_barrier_semaphore()
    for k in range(1, 16):
        pl.semaphore_signal(barrier, inc=1, device_id=(ahead(k), sub), device_id_type=MESH)
    for j in range(1, 8):
        pl.semaphore_signal(barrier, inc=1, device_id=(dp, peer(j)), device_id_type=MESH)

    def fetch(k, carry):
        cache_copy(k).start()
        return carry

    lax.fori_loop(0, 16, fetch, 0)

    def value_copy(h):
        half = value_up.at[h // 2, :, 128 * (h % 2) : 128 * (h % 2) + 128]
        return pltpu.make_async_copy(value_hbm.at[h], half, value_sem)

    for h in range(8):
        value_copy(h).start()

    def value_wait():
        pltpu.make_async_copy(value_up, value_up, value_sem).wait()

    o_out[4] = jnp.zeros((8, 8, DL), jnp.bfloat16)
    o_in[4] = jnp.zeros((7, 8, DL), jnp.bfloat16)

    query_fetch.wait()
    for r in range(4):
        for c in range(4):
            packed[r, 64 * c : 64 * c + 64, :] = queries[r, :, 128 * c : 128 * c + 128]
        packed[r, 256:288, :] = jnp.concatenate(
            [queries[r, :32, 512:576], queries[r, 32:, 512:576]], axis=1
        )

    def select(k, carry):
        q_out[k] = packed[plan_s[ahead(k)]]
        return carry

    lax.fori_loop(1, 16, select, 0)

    def plan_copy(k):
        return remote(plan_v, plan_in.at[k], ps_sem, pr_sem.at[k], (ahead(k), sub))

    def query_copy(k):
        return remote(q_out.at[k], q_in.at[k], qs_sem, qr_sem.at[k], (ahead(k), sub))

    pl.semaphore_wait(barrier, 22)

    def send_query(k, carry):
        query_copy(k).start()
        return carry

    def send_plan(k, carry):
        plan_copy(k).start()
        return carry

    lax.fori_loop(1, 16, send_plan, 0)
    lax.fori_loop(1, 16, send_query, 0)

    q_in[0] = packed[plan_s[dp]]
    plan_in[0] = plan_v[...]

    def send_unit(u):
        for j in range(1, 8):
            to = peer(j)
            remote(
                o_out.at[u, to], o_in.at[u, j - 1], os_sem, or_sem.at[u // 4], (dp, to)
            ).start()

    def send_stat(b):
        s_out[b] = stat[...].reshape(8, 8, 128)
        for j in range(1, 8):
            to = peer(j)
            remote(
                s_out.at[b, to], s_in.at[b, j - 1], ss_sem, sr_sem.at[b], (dp, to)
            ).start()
        stat[...] = jnp.full((64, 128), masked_score, jnp.float32)

    lane = lax.broadcasted_iota(jnp.int32, (64, 128), 1)

    own_copy.wait()
    stat[...] = jnp.full((64, 128), masked_score, jnp.float32)

    def own_step(r, carry):
        weighted, lse = attend(score(queries[r], own[r]), own[r], own_len[r])
        o_out[r] = weighted.astype(jnp.bfloat16).reshape(8, 8, DL)
        stat[...] = jnp.where(lane == 5 * r, lse, stat[...])
        send_unit(r)
        return carry

    lax.fori_loop(0, 4, own_step, 0)
    send_stat(0)

    def prepare(k):
        cache_copy(k).wait()
        query_copy(k).wait_recv()
        plan_copy(k).wait_recv()

    def score_step(k):
        block = q_in[k]
        query = jnp.concatenate(
            [block[64 * c : 64 * c + 64] for c in range(4)]
            + [jnp.concatenate([block[256:288, :64], block[256:288, 64:]], axis=0)],
            axis=1,
        )
        return score(query, cache[k])

    def step(k, t, last):
        if not last:
            prepare(k + 1)
            scores = score_buffer[t]
            score_buffer[1 - t] = score_step(k + 1)
        else:
            scores = score_buffer[t]
        weighted, lse = attend(scores, cache[k], host_len[behind(k)])
        o_out[k + 5] = weighted.astype(jnp.bfloat16).reshape(8, 8, DL)
        lanes = lax.broadcasted_iota(jnp.int32, (1, 16), 1)
        request = jnp.sum(jnp.where(lanes == dp, plan_in[k], 0), axis=1, keepdims=True)
        stat[...] = jnp.where(lane == 4 * ((k + 1) % 4) + request, lse, stat[...])
        send_unit(k + 5)

    def c_copy(k):
        return remote(c_out.at[k + 5], c_in.at[k], cs_sem, cr_sem, (behind(k), sub))

    def combine(b, count=4):
        def all_in(buffer, target, semaphore):
            return pltpu.make_async_copy(buffer.at[pl.ds(0, 7)], target, semaphore)

        all_in(s_out.at[b], s_in.at[b], sr_sem.at[b]).wait()

        def units_in(first, units):
            block = o_in.at[pl.ds(first, units)]
            pltpu.make_async_copy(block, block, or_sem.at[b]).wait()

        if isinstance(b, int):
            units_in(4 * b, count)
        else:

            @pl.when(b == 1)
            def _():
                units_in(5, 3)

            @pl.when(b != 1)
            def _():
                units_in(4 * b, 4)

        logs = [s_out[b, sub]] + [s_in[b, j] for j in range(7)]
        peak = logs[0]
        for value in logs[1:]:
            peak = jnp.maximum(peak, value)
        weights = [jnp.exp2(value - peak) for value in logs]
        total = weights[0]
        for value in weights[1:]:
            total = total + value
        lse = peak + jnp.log2(total)
        weights = [value / total for value in weights]
        for kk in range(count):
            u = 4 * b + kk
            sums = [jnp.zeros((8, DL), jnp.float32) for _ in range(4)]
            for j in range(8):
                piece = (o_out[u, sub] if j == 0 else o_in[u, j - 1]).astype(jnp.float32)
                for r in range(4):
                    at = 4 * kk + r
                    sums[r] = sums[r] + weights[j][:, at : at + 1] * piece
            for r in range(4):
                latent[4 * kk + r] = sums[r]
            c_out[u, 4] = lse if kk == 0 else pltpu.roll(lse, 128 - 4 * kk, 1)
        rows = 4 * count
        for h in range(0, 8, 2):
            both = jnp.concatenate([latent[:rows, h, :], latent[:rows, h + 1, :]], axis=0)
            value = jnp.dot(
                both.astype(jnp.bfloat16), value_up[h // 2], preferred_element_type=jnp.float32
            )
            for kk in range(count):
                at = 4 * kk
                c_out[4 * b + kk, 0:4, h, :] = value[at : at + 4, :128]
                c_out[4 * b + kk, 0:4, h + 1, :] = value[rows + at : rows + at + 4, 128:]

    def send_back(b, count=4):
        for kk in range(count):
            k = 4 * b + kk - 5

            @pl.when(k > 0)
            def _():
                c_copy(k).start()

    cache_copy(0).wait()
    score_buffer[0] = score_step(0)
    step(0, 0, True)
    others = pl.ds(1, 15)
    for k in (1, 2):
        prepare(k)
        score_buffer[0] = score_step(k)
        step(k, 0, True)
    send_stat(1)
    value_wait()
    combine(0)
    prepare(3)
    score_buffer[1] = score_step(3)

    def pair(i, carry):
        step(2 * i + 1, 1, False)
        step(2 * i + 2, 0, False)

        @pl.when(i % 2 == 0)
        def _():
            send_stat(i // 2 + 1)

        return carry

    lax.fori_loop(1, 7, pair, 0)
    step(15, 1, True)
    send_stat(5)

    def late(b, carry):
        combine(b)
        send_back(b)
        return carry

    lax.fori_loop(1, 5, late, 0)
    combine(5, 1)
    send_back(5, 1)

    for block, semaphore in (
        (q_in.at[others], qs_sem),
        (plan_in.at[others], ps_sem),
        (o_in.at[pl.ds(0, 20)], os_sem),
        (s_in, ss_sem),
        (c_in.at[others], cs_sem),
        (c_in.at[others], cr_sem),
    ):
        pltpu.make_async_copy(block, block, semaphore).wait()

    parts = [c_out.at[u] for u in (0, 1, 2, 3, 5)] + [c_in.at[k] for k in range(1, 16)]
    peak = parts[0][4]
    for part in parts[1:]:
        peak = jnp.maximum(peak, part[4])
    total = jnp.zeros((8, 128), jnp.float32)
    sums = [jnp.zeros((8, 128), jnp.float32) for _ in range(4)]
    for part in parts:
        weight = jnp.exp2(part[4] - peak)
        total = total + weight
        for r in range(4):
            sums[r] = sums[r] + weight[:, r : r + 1] * part[r]
    for r in range(4):
        result[r] = (sums[r] / total[:, r : r + 1]).astype(out.dtype)
    out_copy = pltpu.make_async_copy(result, out, query_sem)
    out_copy.start()
    out_copy.wait()


def local(queries, own_cache, own_len, host_cache, host_len, page_plan, value_up):
    bf16, f32 = jnp.bfloat16, jnp.float32
    host = jnp.swapaxes(host_cache, 3, 4).reshape(16, 576, 1024)
    own = jnp.swapaxes(own_cache, 1, 2)
    vmem = pl.BlockSpec(memory_space=pltpu.VMEM)
    smem = pl.BlockSpec(memory_space=pltpu.SMEM)
    anywhere = pl.BlockSpec(memory_space=pl.ANY)
    dma = pltpu.SemaphoreType.DMA
    return pl.pallas_call(
        kernel,
        out_shape=jax.ShapeDtypeStruct((4, 8, 128), bf16),
        in_specs=[smem, smem, smem, vmem, anywhere, anywhere, anywhere, anywhere],
        out_specs=anywhere,
        scratch_shapes=[
            pltpu.VMEM((4, 64, 576), bf16),
            pltpu.VMEM((4, DL, 256), bf16),
            pltpu.VMEM((4, 576, 256), bf16),
            pltpu.VMEM((16, 576, 1024), bf16),
            pltpu.VMEM((4, 288, 128), bf16),
            pltpu.VMEM((16, 288, 128), bf16),
            pltpu.VMEM((16, 288, 128), bf16),
            pltpu.VMEM((16, 1, 16), jnp.int32),
            pltpu.VMEM((21, 8, 8, DL), bf16),
            pltpu.VMEM((21, 7, 8, DL), bf16),
            pltpu.VMEM((64, 128), f32),
            pltpu.VMEM((6, 8, 8, 128), f32),
            pltpu.VMEM((6, 7, 8, 128), f32),
            pltpu.VMEM((2, 64, 1024), f32),
            pltpu.VMEM((16, 8, DL), f32),
            pltpu.VMEM((4, 8, 128), bf16),
            pltpu.VMEM((24, 5, 8, 128), f32),
            pltpu.VMEM((16, 5, 8, 128), f32),
            dma,
            dma,
            dma,
            dma((16,)),
            dma,
            dma((16,)),
            dma,
            dma((16,)),
            dma,
            dma((6,)),
            dma,
            dma((6,)),
            dma,
            dma,
        ],
        compiler_params=pltpu.CompilerParams(
            vmem_limit_bytes=60 * 2**20, collective_id=0, has_side_effects=True
        ),
    )(
        own_len.reshape(4),
        host_len.reshape(16),
        page_plan.reshape(16),
        page_plan.reshape(1, 16),
        queries,
        own,
        host,
        value_up,
    )


def solution(mesh):
    return jax.shard_map(
        local,
        mesh=mesh,
        in_specs=(
            P("dp", None, None),
            P("dp", "sub", None),
            P("dp", "sub"),
            P("dp", "sub", None, None, None),
            P("dp", "sub", None),
            P("dp", "sub", None),
            P("sub", None, None),
        ),
        out_specs=P("dp", "sub", None),
        check_vma=False,
    )
```

```python
import jax
import jax.numpy as jnp
from jax import lax
from jax.experimental import pallas as pl
from jax.experimental.pallas import tpu as pltpu
from jax.sharding import PartitionSpec as P

MESH = pl.DeviceIdType.MESH
DL = 512
scale2 = 192 ** (-0.5) * 1.4426950408889634
masked_score = -1e30


STEPS = [(0, 0), (2, 2), (2, 3), (3, 2), (2, 1), (1, 2), (2, 0), (0, 2)]
STEPS += [(3, 1), (1, 3), (3, 3), (1, 1), (3, 0), (0, 3), (1, 0), (0, 1)]


def offset(k):
    if isinstance(k, int):
        return STEPS[k]
    words = [sum(step[i] << (2 * n) for n, step in enumerate(STEPS)) for i in range(2)]
    words = [jnp.int32(word - (1 << 32) if word >= 1 << 31 else word) for word in words]
    return tuple(lax.shift_right_logical(word, 2 * k) & 3 for word in words)


def score(query, keys):
    return jnp.dot(query, keys, preferred_element_type=jnp.float32)


def attend(scores, keys, length):
    position = lax.broadcasted_iota(jnp.int32, scores.shape, 1)
    scores = jnp.where(position < length, scores, masked_score)
    largest = jnp.max(scores, axis=1, keepdims=True)
    exponent = jnp.exp2((scores - largest) * scale2)
    total = jnp.sum(exponent, axis=1, keepdims=True)
    weighted = lax.dot_general(
        exponent.astype(jnp.bfloat16),
        keys[:DL],
        (((1,), (1,)), ((), ())),
        preferred_element_type=jnp.float32,
    )
    return weighted / total, largest * scale2 + jnp.log2(total)


def kernel(
    own_len,
    host_len,
    plan_s,
    plan_v,
    queries_hbm,
    own_hbm,
    host_hbm,
    value_hbm,
    out,
    queries,
    value_up,
    own,
    cache,
    packed,
    q_out,
    q_in,
    plan_in,
    o_out,
    o_in,
    stat,
    s_out,
    s_in,
    score_buffer,
    latent,
    result,
    c_out,
    c_in,
    query_sem,
    value_sem,
    own_sem,
    cache_sem,
    qs_sem,
    qr_sem,
    ps_sem,
    pr_sem,
    os_sem,
    or_sem,
    ss_sem,
    sr_sem,
    cs_sem,
    cr_sem,
):
    dp, sub = lax.axis_index("dp"), lax.axis_index("sub")
    y, z = dp // 4, dp % 4

    def ahead(k):
        dy, dz = offset(k)
        return ((y + dy) & 3) * 4 + ((z + dz) & 3)

    def behind(k):
        dy, dz = offset(k)
        return ((y + 4 - dy) & 3) * 4 + ((z + 4 - dz) & 3)

    def peer(j):
        return (sub + j) & 7

    def cache_copy(k):
        return pltpu.make_async_copy(host_hbm.at[behind(k)], cache.at[k], cache_sem.at[k])

    def remote(source, target, send, receive, device):
        return pltpu.make_async_remote_copy(
            source, target, send, receive, device_id=device, device_id_type=MESH
        )

    query_fetch = pltpu.make_async_copy(queries_hbm, queries, query_sem)
    query_fetch.start()
    own_copy = pltpu.make_async_copy(own_hbm, own, own_sem)
    own_copy.start()
    barrier = pltpu.get_barrier_semaphore()
    for k in range(1, 16):
        pl.semaphore_signal(barrier, inc=1, device_id=(ahead(k), sub), device_id_type=MESH)
    for j in range(1, 8):
        pl.semaphore_signal(barrier, inc=1, device_id=(dp, peer(j)), device_id_type=MESH)

    def fetch(k, carry):
        cache_copy(k).start()
        return carry

    lax.fori_loop(0, 16, fetch, 0)

    def value_copy(h):
        half = value_up.at[h // 2, :, 128 * (h % 2) : 128 * (h % 2) + 128]
        return pltpu.make_async_copy(value_hbm.at[h], half, value_sem)

    for h in range(8):
        value_copy(h).start()

    def value_wait():
        pltpu.make_async_copy(value_up, value_up, value_sem).wait()

    o_out[4] = jnp.zeros((8, 8, DL), jnp.bfloat16)
    o_in[4] = jnp.zeros((7, 8, DL), jnp.bfloat16)

    query_fetch.wait()
    for r in range(4):
        for c in range(4):
            packed[r, 64 * c : 64 * c + 64, :] = queries[r, :, 128 * c : 128 * c + 128]
        packed[r, 256:288, :] = jnp.concatenate(
            [queries[r, :32, 512:576], queries[r, 32:, 512:576]], axis=1
        )

    def select(k, carry):
        q_out[k] = packed[plan_s[ahead(k)]]
        return carry

    lax.fori_loop(1, 16, select, 0)

    def plan_copy(k):
        return remote(plan_v, plan_in.at[k], ps_sem, pr_sem.at[k], (ahead(k), sub))

    def query_copy(k):
        return remote(q_out.at[k], q_in.at[k], qs_sem, qr_sem.at[k], (ahead(k), sub))

    pl.semaphore_wait(barrier, 22)

    def send_query(k, carry):
        query_copy(k).start()
        return carry

    def send_plan(k, carry):
        plan_copy(k).start()
        return carry

    lax.fori_loop(1, 16, send_plan, 0)
    lax.fori_loop(1, 16, send_query, 0)

    q_in[0] = packed[plan_s[dp]]
    plan_in[0] = plan_v[...]

    def send_unit(u):
        for j in (4, 5, 3, 2, 6, 7, 1):
            to = peer(j)
            remote(
                o_out.at[u, to], o_in.at[u, j - 1], os_sem, or_sem.at[u // 4], (dp, to)
            ).start()

    def send_stat(b):
        s_out[b] = stat[...].reshape(8, 8, 128)
        for j in (4, 5, 3, 2, 6, 7, 1):
            to = peer(j)
            remote(
                s_out.at[b, to], s_in.at[b, j - 1], ss_sem, sr_sem.at[b], (dp, to)
            ).start()
        stat[...] = jnp.full((64, 128), masked_score, jnp.float32)

    lane = lax.broadcasted_iota(jnp.int32, (64, 128), 1)

    own_copy.wait()
    stat[...] = jnp.full((64, 128), masked_score, jnp.float32)

    def own_step(r, carry):
        weighted, lse = attend(score(queries[r], own[r]), own[r], own_len[r])
        o_out[r] = weighted.astype(jnp.bfloat16).reshape(8, 8, DL)
        stat[...] = jnp.where(lane == 5 * r, lse, stat[...])
        send_unit(r)
        return carry

    for r in range(4):
        own_step(r, 0)
    send_stat(0)

    def prepare(k):
        cache_copy(k).wait()
        query_copy(k).wait_recv()
        plan_copy(k).wait_recv()

    def score_step(k):
        block = q_in[k]
        query = jnp.concatenate(
            [block[64 * c : 64 * c + 64] for c in range(4)]
            + [jnp.concatenate([block[256:288, :64], block[256:288, 64:]], axis=0)],
            axis=1,
        )
        return score(query, cache[k])

    def step(k, t, last):
        if not last:
            prepare(k + 1)
            scores = score_buffer[t]
            score_buffer[1 - t] = score_step(k + 1)
        else:
            scores = score_buffer[t]
        weighted, lse = attend(scores, cache[k], host_len[behind(k)])
        o_out[k + 5] = weighted.astype(jnp.bfloat16).reshape(8, 8, DL)
        lanes = lax.broadcasted_iota(jnp.int32, (1, 16), 1)
        request = jnp.sum(jnp.where(lanes == dp, plan_in[k], 0), axis=1, keepdims=True)
        stat[...] = jnp.where(lane == 4 * ((k + 1) % 4) + request, lse, stat[...])
        send_unit(k + 5)

    def c_copy(k):
        return remote(c_out.at[k + 5], c_in.at[k], cs_sem, cr_sem, (behind(k), sub))

    def combine(b, count=4):
        def all_in(buffer, target, semaphore):
            return pltpu.make_async_copy(buffer.at[pl.ds(0, 7)], target, semaphore)

        all_in(s_out.at[b], s_in.at[b], sr_sem.at[b]).wait()

        def units_in(first, units):
            block = o_in.at[pl.ds(first, units)]
            pltpu.make_async_copy(block, block, or_sem.at[b]).wait()

        if isinstance(b, int):
            units_in(4 * b, count)
        else:

            @pl.when(b == 1)
            def _():
                units_in(5, 3)

            @pl.when(b != 1)
            def _():
                units_in(4 * b, 4)

        logs = [s_out[b, sub]] + [s_in[b, j] for j in range(7)]
        peak = logs[0]
        for value in logs[1:]:
            peak = jnp.maximum(peak, value)
        weights = [jnp.exp2(value - peak) for value in logs]
        total = weights[0]
        for value in weights[1:]:
            total = total + value
        lse = peak + jnp.log2(total)
        weights = [value / total for value in weights]
        for kk in range(count):
            u = 4 * b + kk
            sums = [jnp.zeros((8, DL), jnp.float32) for _ in range(4)]
            for j in range(8):
                piece = (o_out[u, sub] if j == 0 else o_in[u, j - 1]).astype(jnp.float32)
                for r in range(4):
                    at = 4 * kk + r
                    sums[r] = sums[r] + weights[j][:, at : at + 1] * piece
            for r in range(4):
                latent[4 * kk + r] = sums[r]
            c_out[u, 4] = lse if kk == 0 else pltpu.roll(lse, 128 - 4 * kk, 1)
        rows = 4 * count
        for h in range(0, 8, 2):
            both = jnp.concatenate([latent[:rows, h, :], latent[:rows, h + 1, :]], axis=0)
            value = jnp.dot(
                both.astype(jnp.bfloat16), value_up[h // 2], preferred_element_type=jnp.float32
            )
            for kk in range(count):
                at = 4 * kk
                c_out[4 * b + kk, 0:4, h, :] = value[at : at + 4, :128]
                c_out[4 * b + kk, 0:4, h + 1, :] = value[rows + at : rows + at + 4, 128:]

    def send_back(b, count=4):
        for kk in range(count):
            k = 4 * b + kk - 5

            @pl.when(k > 0)
            def _():
                c_copy(k).start()

    cache_copy(0).wait()
    score_buffer[0] = score_step(0)
    step(0, 0, True)
    others = pl.ds(1, 15)
    for k in (1, 2):
        prepare(k)
        score_buffer[0] = score_step(k)
        step(k, 0, True)
    send_stat(1)
    value_wait()
    combine(0)
    prepare(3)
    score_buffer[1] = score_step(3)

    def pair(i, carry):
        step(2 * i + 1, 1, False)
        step(2 * i + 2, 0, False)

        @pl.when(i % 2 == 0)
        def _():
            send_stat(i // 2 + 1)

        return carry

    lax.fori_loop(1, 7, pair, 0)
    step(15, 1, True)
    send_stat(5)

    def late(b, carry):
        combine(b)
        send_back(b)
        return carry

    lax.fori_loop(1, 5, late, 0)
    combine(5, 1)
    send_back(5, 1)

    for block, semaphore in (
        (q_in.at[others], qs_sem),
        (plan_in.at[others], ps_sem),
        (o_in.at[pl.ds(0, 20)], os_sem),
        (s_in, ss_sem),
        (c_in.at[others], cs_sem),
        (c_in.at[others], cr_sem),
    ):
        pltpu.make_async_copy(block, block, semaphore).wait()

    parts = [c_out.at[u] for u in (0, 1, 2, 3, 5)] + [c_in.at[k] for k in range(1, 16)]
    peak = parts[0][4]
    for part in parts[1:]:
        peak = jnp.maximum(peak, part[4])
    total = jnp.zeros((8, 128), jnp.float32)
    sums = [jnp.zeros((8, 128), jnp.float32) for _ in range(4)]
    for part in parts:
        weight = jnp.exp2(part[4] - peak)
        total = total + weight
        for r in range(4):
            sums[r] = sums[r] + weight[:, r : r + 1] * part[r]
    for r in range(4):
        result[r] = (sums[r] / total[:, r : r + 1]).astype(out.dtype)
    out_copy = pltpu.make_async_copy(result, out, query_sem)
    out_copy.start()
    out_copy.wait()


def local(queries, own_cache, own_len, host_cache, host_len, page_plan, value_up):
    bf16, f32 = jnp.bfloat16, jnp.float32
    host = jnp.swapaxes(host_cache, 3, 4).reshape(16, 576, 1024)
    own = jnp.swapaxes(own_cache, 1, 2)
    vmem = pl.BlockSpec(memory_space=pltpu.VMEM)
    smem = pl.BlockSpec(memory_space=pltpu.SMEM)
    anywhere = pl.BlockSpec(memory_space=pl.ANY)
    dma = pltpu.SemaphoreType.DMA
    return pl.pallas_call(
        kernel,
        out_shape=jax.ShapeDtypeStruct((4, 8, 128), bf16),
        in_specs=[smem, smem, smem, vmem, anywhere, anywhere, anywhere, anywhere],
        out_specs=anywhere,
        scratch_shapes=[
            pltpu.VMEM((4, 64, 576), bf16),
            pltpu.VMEM((4, DL, 256), bf16),
            pltpu.VMEM((4, 576, 256), bf16),
            pltpu.VMEM((16, 576, 1024), bf16),
            pltpu.VMEM((4, 288, 128), bf16),
            pltpu.VMEM((16, 288, 128), bf16),
            pltpu.VMEM((16, 288, 128), bf16),
            pltpu.VMEM((16, 1, 16), jnp.int32),
            pltpu.VMEM((21, 8, 8, DL), bf16),
            pltpu.VMEM((21, 7, 8, DL), bf16),
            pltpu.VMEM((64, 128), f32),
            pltpu.VMEM((6, 8, 8, 128), f32),
            pltpu.VMEM((6, 7, 8, 128), f32),
            pltpu.VMEM((2, 64, 1024), f32),
            pltpu.VMEM((16, 8, DL), f32),
            pltpu.VMEM((4, 8, 128), bf16),
            pltpu.VMEM((24, 5, 8, 128), f32),
            pltpu.VMEM((16, 5, 8, 128), f32),
            dma,
            dma,
            dma,
            dma((16,)),
            dma,
            dma((16,)),
            dma,
            dma((16,)),
            dma,
            dma((6,)),
            dma,
            dma((6,)),
            dma,
            dma,
        ],
        compiler_params=pltpu.CompilerParams(
            vmem_limit_bytes=60 * 2**20, collective_id=0, has_side_effects=True
        ),
    )(
        own_len.reshape(4),
        host_len.reshape(16),
        page_plan.reshape(16),
        page_plan.reshape(1, 16),
        queries,
        own,
        host,
        value_up,
    )


def solution(mesh):
    return jax.shard_map(
        local,
        mesh=mesh,
        in_specs=(
            P("dp", None, None),
            P("dp", "sub", None),
            P("dp", "sub"),
            P("dp", "sub", None, None, None),
            P("dp", "sub", None),
            P("dp", "sub", None),
            P("sub", None, None),
        ),
        out_specs=P("dp", "sub", None),
        check_vma=False,
    )
```
